32 devices in a mesh: sample: 8 (over y, x, core), token: 4 (over z).
Axes of the slice: x: 2, y: 2, z: 4, core: 2. Of those that a mesh axis runs over, the one named last changes fastest.
Arguments:
- activations: bfloat16 [16, 416, 768], P('sample', 'token'), may hold values from -6 to 6
- single: bfloat16 [416, 384], P('token'), may hold values from -6 to 6
- noise_index: int32 [16], P('sample'), may hold values from 0 to 199
- token_mask: int32 [416], replicated, may hold values 0 or 1
- pair_bias: bfloat16 [416, 16, 416], P('token', None, 'sample'), may hold values from -36 to 400
- fourier_freq: float32 [256], replicated, may hold values from -5 to 5
- fourier_phase: float32 [256], replicated, may hold values from 0 to 1
- noise_weight: bfloat16 [256, 384], replicated, may hold values from -0.375 to 0.375
- ada_weight: bfloat16 [384, 2304], replicated, may hold values from -0.3125 to 0.3125
- qkvg_weight: bfloat16 [768, 3072], P(None, 'sample'), may hold values from -0.21875 to 0.21875
- out_weight: bfloat16 [768, 768], P(None, 'sample'), may hold values from -0.21875 to 0.21875
Outputs:
- updated: bfloat16 [16, 416, 768], P('sample', 'token')
The draws below stay inside these ranges and needn't reach their ends.
All inputs are finite; a program needn't handle non-finite values.
Results may differ from the reference program's by a relative error of at most 0.008.
Values may be sent and summed in bfloat16 or wider, within the bound.
No kernel may reach another device: no remote copies, remote signals or barrier semaphores. Data moves between devices by JAX's collectives and lax.ppermute only.
A program may use at most 128 MiB of HBM per device.

```python
import math
import jax
import jax.numpy as jnp
from jax import lax

D = 768
HEADS = 16
C_S = 384
FOURIER = 256
STEPS = 200
TOKENS = 416
SAMPLES = 16


def draw_pair_bias(key, part):
    streams = jax.random.split(jax.random.fold_in(key, 17), 4)
    full_shape = (TOKENS, HEADS, TOKENS)
    row_scale = jnp.exp(jax.random.uniform(streams[0], (TOKENS, 1, 1), jnp.float32, math.log(0.3), math.log(3.0)))
    col_scale = jnp.exp(jax.random.uniform(streams[1], (1, 1, TOKENS), jnp.float32, math.log(0.3), math.log(3.0)))
    base_draw = jax.random.normal(streams[3], full_shape, jnp.float32)
    drawn = jnp.clip(base_draw, -4.0, 4.0) * row_scale * col_scale
    return drawn.astype(jnp.bfloat16)


def touch_ends(values, rng, least, high):
    index_at = [jax.random.randint(jax.random.fold_in(rng, axis), (), 0, length) for axis, length in enumerate(values.shape)]
    main_axis = values.shape.index(max(values.shape))
    beside = index_at[:main_axis] + [(index_at[main_axis] + 1) % values.shape[main_axis]] + index_at[main_axis + 1:]
    return values.at[tuple(index_at)].set(least).at[tuple(beside)].set(high)


def block_scale(own_key, extent, shards, smallest, top_value):
    def one(dim, shards_of):
        steps = jax.random.uniform(jax.random.fold_in(jax.random.fold_in(own_key, 6), dim), (shards_of,), jnp.float32, smallest / len(shards), top_value / len(shards))
        return jnp.repeat(jnp.exp(steps), extent[dim] // shards_of).reshape((-1,) + (1,) * (len(extent) - dim - 1))

    gain = one(*shards[0])
    for cut in shards[1:]:
        gain = gain * one(*cut)
    return gain


def bell_draw(own_key, dims, scale, most, cuts=(), kind=jnp.bfloat16):
    gain = block_scale(own_key, dims, cuts, -0.22, 0.18) if cuts else 1.0
    values = jax.random.normal(own_key, dims, jnp.float32) * scale * gain
    return jnp.minimum(jnp.maximum(values, -most), most).astype(kind)


def setup_inputs(seed: int = 0) -> dict:
    arg_keys = jax.random.split(jax.random.key(seed), 12)
    activations = bell_draw(arg_keys[0], (SAMPLES, TOKENS, D), 1.0, 6.0, ((0, 8), (1, 4)))
    single = bell_draw(arg_keys[1], (TOKENS, C_S), 1.0, 6.0, ((0, 4),))
    noise_index = touch_ends(jax.random.randint(arg_keys[2], (SAMPLES,), 0, STEPS), jax.random.fold_in(arg_keys[2], 1), 0, STEPS - 1).astype(jnp.int32)
    token_mask = touch_ends((jax.random.randint(arg_keys[3], (TOKENS,), 0, 8) < 7).astype(jnp.int32), jax.random.fold_in(arg_keys[3], 1), 0, 1)
    pair_bias = draw_pair_bias(jax.random.fold_in(arg_keys[11], 71), 0)
    fourier_freq = bell_draw(arg_keys[5], (FOURIER,), 1.0, 5.0, (), jnp.float32)
    fourier_phase = jnp.clip(jax.random.uniform(arg_keys[6], (FOURIER,), jnp.float32, 0.0, 1.0), 0.0, 1.0)
    noise_weight = bell_draw(arg_keys[7], (FOURIER, C_S), FOURIER ** -0.5, 0.375)
    ada_weight = bell_draw(arg_keys[8], (C_S, 3 * D), C_S ** -0.5, 0.3125)
    qkvg_weight = bell_draw(arg_keys[9], (D, 4 * D), D ** -0.5, 0.21875, ((1, 8),))
    out_weight = bell_draw(arg_keys[10], (D, D), D ** -0.5, 0.21875, ((1, 8),))
    return {"activations": activations, "single": single, "noise_index": noise_index, "token_mask": token_mask, "pair_bias": pair_bias, "fourier_freq": fourier_freq, "fourier_phase": fourier_phase, "noise_weight": noise_weight, "ada_weight": ada_weight, "qkvg_weight": qkvg_weight, "out_weight": out_weight}


sigma_data = 16.0
sigma_top = 160.0
sigma_low = 0.0004
exponent = 7.0
mask_penalty = 1000000000.0
norm_eps = 1e-05

def layer_norm(values):
    center = lax.optimization_barrier(jnp.mean(values, axis=-1, keepdims=True))
    deviation = values - center
    spread = lax.optimization_barrier(jnp.mean(deviation * deviation, axis=-1, keepdims=True))
    return deviation * lax.rsqrt(spread + norm_eps)

def noise_embedding(noise_index, fourier_freq, fourier_phase, noise_weight):
    fraction = noise_index.astype(jnp.float32) / (STEPS - 1)
    top_root = sigma_top ** (1.0 / exponent)
    low_root = sigma_low ** (1.0 / exponent)
    level_base = top_root + fraction * (low_root - top_root)
    sigma_level = sigma_data * level_base ** exponent
    log_level = 0.25 * jnp.log(sigma_level / sigma_data)
    angles = 2.0 * math.pi * (log_level[:, None] * fourier_freq[None, :] + fourier_phase[None, :])
    features = layer_norm(jnp.cos(angles)).astype(jnp.bfloat16)
    return jnp.dot(features, noise_weight, preferred_element_type=jnp.float32)

def reference(activations, single, noise_index, token_mask, pair_bias, fourier_freq, fourier_phase, noise_weight, ada_weight, qkvg_weight, out_weight):
    head_size = D // HEADS
    inverse = 1.0 / math.sqrt(head_size)
    penalty = (token_mask.astype(jnp.float32) - 1.0) * mask_penalty
    bias_float = pair_bias.astype(jnp.float32)
    embedded = noise_embedding(noise_index, fourier_freq, fourier_phase, noise_weight)

    def one_sample(inputs):
        tokens_in, embed_row = inputs
        condition = layer_norm(single.astype(jnp.float32) + embed_row[None, :]).astype(jnp.bfloat16)
        modulate = jnp.dot(condition, ada_weight, preferred_element_type=jnp.float32)
        scale_part = modulate[:, :D]
        shift_part = modulate[:, D:2 * D]
        out_gate = modulate[:, 2 * D:]
        normed = (jax.nn.sigmoid(scale_part) * layer_norm(tokens_in.astype(jnp.float32)) + shift_part).astype(jnp.bfloat16)
        projected = lax.optimization_barrier(jnp.dot(normed, qkvg_weight, preferred_element_type=jnp.float32).astype(jnp.bfloat16))
        widened = projected.astype(jnp.float32)
        queries = widened[:, :D].reshape(TOKENS, HEADS, head_size)
        keys_all = widened[:, D:2 * D].reshape(TOKENS, HEADS, head_size)
        values_all = widened[:, 2 * D:3 * D].reshape(TOKENS, HEADS, head_size)
        scores = jnp.einsum('qhe,khe->qhk', queries, keys_all) * inverse + bias_float + penalty[None, None, :]
        row_top = lax.optimization_barrier(jnp.max(scores, axis=-1, keepdims=True))
        weights = jnp.exp(scores - row_top)
        row_total = lax.optimization_barrier(jnp.sum(weights, axis=-1))
        rounded = lax.optimization_barrier(weights.astype(jnp.bfloat16)).astype(jnp.float32)
        attended = jnp.einsum('qhk,khe->qhe', rounded, values_all) / row_total[:, :, None]
        gated_rows = (attended.reshape(TOKENS, D) * jax.nn.sigmoid(widened[:, 3 * D:])).astype(jnp.bfloat16)
        output = jnp.dot(gated_rows, out_weight, preferred_element_type=jnp.float32)
        return (jax.nn.sigmoid(out_gate) * output).astype(jnp.bfloat16)
    return lax.map(one_sample, (activations, embedded))
```

```python
import functools
import math

import jax
import jax.numpy as jnp
from jax import lax
from jax.experimental import pallas as pl
from jax.experimental.pallas import tpu as pltpu
from jax.sharding import PartitionSpec as P

HEADS = 16
STEPS = 200

sigma_data = 16.0
sigma_top = 160.0
sigma_low = 0.0004
exponent = 7.0
mask_penalty = 1000000000.0
norm_eps = 1e-05

VMEM = pl.BlockSpec(memory_space=pltpu.VMEM)
SMEM = pl.BlockSpec(memory_space=pltpu.SMEM)
ANY = pl.BlockSpec(memory_space=pl.ANY)


def layer_norm(values):
    center = jnp.mean(values, axis=-1, keepdims=True)
    deviation = values - center
    spread = jnp.mean(deviation * deviation, axis=-1, keepdims=True)
    return deviation * lax.rsqrt(spread + norm_eps)


def xor_send(x, axis, size, flip):
    return lax.ppermute(x, axis, [(i, i ^ flip) for i in range(size)])


def noise_rows(index_ref, freq, phase, samples):
    rows = lax.broadcasted_iota(jnp.int32, (8, 1), 0)
    index = jnp.zeros((8, 1), jnp.float32)
    for b in range(samples):
        index = jnp.where(rows == b, index_ref[b].astype(jnp.float32), index)
    fraction = index / (STEPS - 1)
    top_root = sigma_top ** (1.0 / exponent)
    low_root = sigma_low ** (1.0 / exponent)
    base = top_root + fraction * (low_root - top_root)
    square = base * base
    power = square * square * square * base
    log_level = 0.25 * jnp.log(power)
    turns = log_level * freq + phase
    return layer_norm(jnp.cos(2.0 * math.pi * turns)).astype(jnp.bfloat16)


def modulate_kernel(samples, index_ref, act_ref, single_ref, freq_ref, phase_ref, noise_w_ref, ada_ref, normed_ref, cond_ref):
    tokens, width = act_ref.shape[1:]
    features = noise_rows(index_ref, freq_ref[...], phase_ref[...], samples)
    embedded = jnp.dot(features, noise_w_ref[...], preferred_element_type=jnp.float32)
    single = single_ref[...].astype(jnp.float32)
    cond = jnp.concatenate([layer_norm(single + embedded[b : b + 1]) for b in range(samples)], axis=0)
    cond = cond.astype(jnp.bfloat16)
    cond_ref[...] = cond
    act = jnp.concatenate([layer_norm(act_ref[b].astype(jnp.float32)) for b in range(samples)], axis=0)
    scale = jnp.dot(cond, ada_ref[:, :width], preferred_element_type=jnp.float32)
    shift = jnp.dot(cond, ada_ref[:, width:], preferred_element_type=jnp.float32)
    normed_ref[...] = (jax.nn.sigmoid(scale) * act + shift).astype(jnp.bfloat16)


def bias_kernel(groups, heads_in, side_ref, own_ref, other_ref, out_ref, own_f, other_f):
    side = side_ref[0]
    own_f[...] = own_ref[...].astype(jnp.float32)
    other_f[...] = other_ref[...].astype(jnp.float32)
    for k in range(groups * heads_in):
        h = (k // heads_in) * 2 * heads_in + k % heads_in + side * heads_in
        a = own_f[:, h, :]
        b = other_f[:, h, :]
        low = jnp.where(side == 0, a, b)
        high = jnp.where(side == 0, b, a)
        pad = jnp.zeros((low.shape[0], out_ref.shape[2] - 2 * low.shape[1]), jnp.float32)
        out_ref[k] = jnp.concatenate([low, high, pad], axis=1).astype(jnp.bfloat16)


def attention_kernel(cfg, place_ref, mask_ref, *refs):
    blocks, groups, heads_in, head, inverse, weight_parts, samples = (
        cfg["blocks"], cfg["groups"], cfg["heads_in"], cfg["head"], cfg["inverse"], cfg["weight_parts"], cfg["samples"],
    )
    chips = 4 * groups
    it = iter(refs)
    own = [next(it) for _ in range(blocks)]
    other = [next(it) for _ in range(blocks)]
    weights = [[next(it) for _ in range(weight_parts[d])] for d in range(chips)]
    bias = [next(it) for _ in range(blocks)]
    own_out, other_out = next(it), next(it)
    n_s, w_s, b_s, k_s, v_s, sem = [next(it) for _ in range(6)]
    chip, token = place_ref[0], place_ref[1]
    rows, width = own[0].shape
    tokens = rows // samples
    cols = heads_in * head
    key_pad = b_s.shape[-1]

    copies = []
    for d in range(chips):
        start = 0
        for part in weights[d]:
            size = part.shape[0]
            copies.append(pltpu.make_async_copy(part, w_s.at[chip ^ d, pl.ds(start, size)], sem))
            start += size
    for d in range(blocks):
        copies.append(pltpu.make_async_copy(own[d], n_s.at[d, 0], sem))
        copies.append(pltpu.make_async_copy(other[d], n_s.at[d, 1], sem))
        copies.append(pltpu.make_async_copy(bias[d], b_s.at[token ^ chip ^ d], sem))
    for c in copies:
        c.start()
    k_s[...] = jnp.zeros_like(k_s)
    v_s[...] = jnp.zeros_like(v_s)
    lane = lax.broadcasted_iota(jnp.int32, (1, cols), 1) // head
    key_lane = lax.broadcasted_iota(jnp.int32, (1, key_pad), 1)
    penalty = []
    for p in range(blocks):
        row = (mask_ref[pl.ds(token ^ p, 1), :].astype(jnp.float32) - 1.0) * mask_penalty
        penalty.append(jnp.where(key_lane < tokens, row, -1e30))
    for c in copies:
        c.wait()
    for j in range(groups):
        for p in range(blocks):
            x = n_s[p].reshape(2 * rows, width)
            k = jnp.dot(x, w_s[groups + j], preferred_element_type=jnp.float32)
            v = jnp.dot(x, w_s[2 * groups + j], preferred_element_type=jnp.float32)
            for b in range(2 * samples):
                k_s[b, p * key_pad : p * key_pad + tokens] = k[b * tokens : (b + 1) * tokens].astype(jnp.bfloat16)
                v_s[b, p * key_pad : p * key_pad + tokens] = v[b * tokens : (b + 1) * tokens].astype(jnp.bfloat16)
        x = n_s[0].reshape(2 * rows, width)
        q = jnp.dot(x, w_s[j], preferred_element_type=jnp.float32)
        g = jnp.dot(x, w_s[3 * groups + j], preferred_element_type=jnp.float32).astype(jnp.bfloat16).astype(jnp.float32)
        gate = jax.nn.sigmoid(g)
        results = []
        for b in range(2 * samples):
            qb = q[b * tokens : (b + 1) * tokens]
            stacked = jnp.concatenate([jnp.where(lane == h, qb, 0.0) for h in range(heads_in)], axis=0).astype(jnp.bfloat16)
            scores = lax.dot_general(stacked, k_s[b], (((1,), (1,)), ((), ())), preferred_element_type=jnp.float32)
            parts = []
            for p in range(blocks):
                bias_rows = b_s[p, j * heads_in : (j + 1) * heads_in].astype(jnp.float32).reshape(heads_in * tokens, key_pad)
                parts.append(scores[:, p * key_pad : (p + 1) * key_pad] * inverse + bias_rows + penalty[p])
            top = functools.reduce(jnp.maximum, parts)
            top = jnp.max(top, axis=-1, keepdims=True)
            exps = [jnp.exp(s - top) for s in parts]
            total = jnp.sum(functools.reduce(jnp.add, exps), axis=-1, keepdims=True)
            probs = jnp.concatenate([e.astype(jnp.bfloat16) for e in exps], axis=1)
            mixed = jnp.dot(probs, v_s[b], preferred_element_type=jnp.float32) / total
            attended = jnp.zeros((tokens, cols), jnp.float32)
            for h in range(heads_in):
                attended = jnp.where(lane == h, mixed[h * tokens : (h + 1) * tokens], attended)
            results.append(attended * gate[b * tokens : (b + 1) * tokens])
        own_out[j] = jnp.concatenate(results[:samples], axis=0).astype(jnp.bfloat16)
        other_out[j] = jnp.concatenate(results[samples:], axis=0).astype(jnp.bfloat16)


def chip_gather(x, n_s):
    chips = n_s // 2
    if chips == 4 and x.shape[0] % 32 == 0:
        half = x.shape[0] // 2
        near = xor_send(x, "sample", n_s, 2)
        side = xor_send(x, "sample", n_s, 4)
        low = xor_send(near[:half], "sample", n_s, 4)
        high = xor_send(side[half:], "sample", n_s, 2)
        return [[x], [near], [side], [low, high]]
    return [[x]] + [[xor_send(x, "sample", n_s, 2 * d)] for d in range(1, chips)]


def token_gather(x, n_t):
    if n_t != 4:
        return [x] + [xor_send(x, "token", n_t, d) for d in range(1, n_t)]
    two = xor_send(x, "token", n_t, 2)
    one = xor_send(x, "token", n_t, 1)
    middle = lax.ppermute(x, "token", [(1, 2), (2, 1)])
    ends = lax.ppermute(two, "token", [(2, 3), (1, 0)])
    return [x, one, two, middle + ends]


def body(
    activations,
    single,
    noise_index,
    token_mask,
    pair_bias,
    fourier_freq,
    fourier_phase,
    noise_weight,
    ada_weight,
    qkvg_weight,
    out_weight,
    n_s,
    n_t,
):
    samples, tokens, width = activations.shape
    head = width // HEADS
    shard_cols = qkvg_weight.shape[1]
    chips = n_s // 2
    groups = chips // 4
    heads_in = shard_cols // head
    rows = samples * tokens
    s = lax.axis_index("sample")
    t = lax.axis_index("token")
    side = s % 2
    place = jnp.stack([s // 2, t]).astype(jnp.int32)

    weight_pieces = chip_gather(qkvg_weight, n_s)
    bias_other = xor_send(pair_bias, "sample", n_s, 1)

    normed, condition = pl.pallas_call(
        functools.partial(modulate_kernel, samples),
        out_shape=(
            jax.ShapeDtypeStruct((rows, width), jnp.bfloat16),
            jax.ShapeDtypeStruct((rows, single.shape[1]), jnp.bfloat16),
        ),
        grid=(1,),
        in_specs=[SMEM, VMEM, VMEM, VMEM, VMEM, VMEM, pl.BlockSpec((single.shape[1], 2 * width), lambda i: (0, 0))],
        out_specs=(VMEM, VMEM),
        name="modulate",
    )(noise_index, activations, single, fourier_freq[None], fourier_phase[None], noise_weight, ada_weight)

    own_blocks = token_gather(normed, n_t)
    other_blocks = [xor_send(x, "sample", n_s, 1) for x in own_blocks]

    key_pad = -(-tokens // 128) * 128
    local_bias = pl.pallas_call(
        functools.partial(bias_kernel, groups, heads_in),
        out_shape=jax.ShapeDtypeStruct((groups * heads_in, tokens, key_pad), jnp.bfloat16),
        in_specs=[SMEM, VMEM, VMEM],
        out_specs=VMEM,
        scratch_shapes=[pltpu.VMEM(pair_bias.shape, jnp.float32)] * 2,
        name="bias_order",
    )(side[None].astype(jnp.int32), pair_bias, bias_other)
    bias_pieces = [local_bias] + [xor_send(local_bias, "sample", n_s, 2 * d) for d in range(1, chips)]

    blocks = n_t
    cfg = {
        "blocks": blocks, "groups": groups, "heads_in": heads_in, "head": head, "inverse": 1.0 / math.sqrt(head),
        "weight_parts": [len(p) for p in weight_pieces], "samples": samples,
    }
    mask_rows = jnp.pad(token_mask.reshape(n_t, tokens), ((0, 0), (0, key_pad - tokens)))
    gated_own, gated_other = pl.pallas_call(
        functools.partial(attention_kernel, cfg),
        out_shape=(jax.ShapeDtypeStruct((groups, rows, shard_cols), jnp.bfloat16),) * 2,
        in_specs=[SMEM, VMEM] + [ANY] * (2 * blocks + sum(cfg["weight_parts"]) + blocks),
        out_specs=(VMEM, VMEM),
        scratch_shapes=[
            pltpu.VMEM((blocks, 2, rows, width), jnp.bfloat16),
            pltpu.VMEM((chips, width, shard_cols), jnp.bfloat16),
            pltpu.VMEM((blocks, groups * heads_in, tokens, key_pad), jnp.bfloat16),
            pltpu.VMEM((2 * samples, blocks * key_pad, shard_cols), jnp.bfloat16),
            pltpu.VMEM((2 * samples, blocks * key_pad, shard_cols), jnp.bfloat16),
            pltpu.SemaphoreType.DMA,
        ],
        name="attention",
    )(place, mask_rows, *own_blocks, *other_blocks, *[x for p in weight_pieces for x in p], *bias_pieces)

    gated_back = xor_send(gated_other, "sample", n_s, 1)
    first = jnp.where(side == 0, gated_own, gated_back)
    second = jnp.where(side == 0, gated_back, gated_own)
    gated_rows = jnp.stack([first, second], axis=1).reshape(2 * groups, rows, shard_cols)
    gated_rows = jnp.moveaxis(gated_rows, 0, 1).reshape(rows, width)

    out_turned = out_weight.T
    out_pair = xor_send(out_turned, "sample", n_s, 1)
    out_both = jnp.concatenate([jnp.where(side == 0, out_turned, out_pair), jnp.where(side == 0, out_pair, out_turned)], axis=0)
    out_pieces = [out_both] + [xor_send(out_both, "sample", n_s, 2 * d) for d in range(1, chips)]
    order = jnp.arange(chips) ^ (s // 2)
    out_full = jnp.stack(out_pieces)[order].reshape(width, width)
    out_gate = jnp.dot(condition, ada_weight[:, 2 * width :], preferred_element_type=jnp.float32)
    output = (
        jax.nn.sigmoid(out_gate)
        * lax.dot_general(gated_rows, out_full, (((1,), (1,)), ((), ())), preferred_element_type=jnp.float32)
    ).astype(jnp.bfloat16)
    return output.reshape(samples, tokens, width)


def solution(mesh):
    placed = (
        P("sample", "token", None),
        P("token", None),
        P("sample"),
        P(),
        P("token", None, "sample"),
        P(),
        P(),
        P(),
        P(),
        P(None, "sample"),
        P(None, "sample"),
    )
    run = functools.partial(body, n_s=mesh.shape["sample"], n_t=mesh.shape["token"])
    return jax.shard_map(run, mesh=mesh, in_specs=placed, out_specs=P("sample", "token", None), check_vma=False)
```
